128 devices in a mesh: lm: 8 (over z, x_hi), sl: 16 (over y, x_lo, core).
Axes of the slice: x: 4 (x_hi: 2, x_lo: 2; x = x_hi * 2 + x_lo), y: 4, z: 4, core: 2. Of those that a mesh axis runs over, the one named last changes fastest.
Arguments:
- slab: bfloat16 [16384, 1024], P('sl'), may hold values from -6 to 6
- landmarks: bfloat16 [32768, 1024], P(('lm', 'sl')), may hold values from -6 to 6
- codes: bfloat16 [32768, 96], P(('lm', 'sl')), may hold values from -4 to 4
- exponents: int32 [256], P(('lm', 'sl')), may hold values from -3 to 3
- eigvec: bfloat16 [96, 64], replicated, may hold values from -0.625 to 0.625
- ritz: float32 [64], replicated, may hold values from 0.5 to 4
Outputs:
- extended: float32 [16384, 64], P('sl')
The draws below stay inside these ranges and needn't reach their ends.
All inputs are finite; a program needn't handle non-finite values.
Results may differ from the reference program's by a relative error of at most 0.004.
Values may be sent and summed in bfloat16 or wider, within the bound.
A program may use at most 128 MiB of HBM per device.

```python
import math
import jax
import jax.numpy as jnp
from jax import lax

FEAT = 1024
BASIS = 96
RITZ = 64
BLOCK = 128
LM_DEV = 256
NL = 32768
SLAB = 16384


def with_ends(result, stream_key, smallest, top_value):
    extent = result.shape
    spot = [jax.random.randint(jax.random.fold_in(stream_key, axis), (), 0, extent[axis]) for axis in range(len(extent))]
    result = result.at[tuple(spot)].set(smallest)
    longest = extent.index(max(extent))
    spot[longest] = (spot[longest] + 1) % extent[longest]
    return result.at[tuple(spot)].set(top_value)


def shard_levels(key, dims, split, smallest, high):
    loudness = 1.0
    for axis_at, blocks in split:
        heights = jax.random.uniform(jax.random.fold_in(jax.random.fold_in(key, 6), axis_at), (blocks,), jnp.float32, smallest / len(split), high / len(split))
        loudness = loudness * jnp.repeat(jnp.exp(heights), dims[axis_at] // blocks).reshape((-1,) + (1,) * (len(dims) - 1 - axis_at))
    return loudness


def centred(stream_key, extent, deviation, bound, split=(), dtype=jnp.bfloat16):
    values = jax.random.normal(stream_key, extent, jnp.float32) * deviation
    if len(split) > 0:
        values = shard_levels(stream_key, extent, split, -0.22, 0.18) * values
    return jnp.clip(values, min=-bound, max=bound).astype(dtype)


def setup_inputs(seed: int = 0) -> dict:
    seeds = jax.random.split(jax.random.key(seed), 7)
    slab = centred(seeds[0], (SLAB, FEAT), 1.0, 6.0, ((0, 16),))
    landmarks = centred(seeds[1], (NL, FEAT), 1.0, 6.0, ((0, 128),))
    codes = centred(seeds[2], (NL, BASIS), 1.0, 4.0, ((0, 128),))
    exponents = with_ends(jax.random.randint(seeds[3], (NL // BLOCK,), -3, 4), jax.random.fold_in(seeds[3], 1), -3, 3).astype(jnp.int32)
    eigvec = centred(seeds[4], (BASIS, RITZ), BASIS ** -0.5, 0.625)
    ritz = jnp.clip(jnp.exp(jax.random.uniform(seeds[5], (RITZ,), jnp.float32, math.log(0.5), math.log(4.0))), 0.5, 4.0)
    return {"slab": slab, "landmarks": landmarks, "codes": codes, "exponents": exponents, "eigvec": eigvec, "ritz": ritz}


def reference(slab, landmarks, codes, exponents, eigvec, ritz):
    scale = jnp.exp2(exponents.astype(jnp.float32))
    rows_scale = jnp.repeat(scale, BLOCK)
    basis = (codes.astype(jnp.float32) * rows_scale[:, None]).astype(jnp.bfloat16)
    vectors = jnp.dot(basis, eigvec, preferred_element_type=jnp.float32).astype(jnp.bfloat16)
    factor = 1.0 / (ritz * math.sqrt(NL))
    coeff = 1.0 / math.sqrt(FEAT)
    width = LM_DEV
    count = NL // width
    land_blocks = landmarks.reshape(count, width, FEAT)
    vec_blocks = vectors.reshape(count, width, RITZ)

    def step(total, pieces):
        land_piece, vec_piece = pieces
        scores = jnp.dot(slab, land_piece.T, preferred_element_type=jnp.float32) * coeff
        affinity = jnp.exp(scores).astype(jnp.bfloat16)
        return (total + jnp.dot(affinity, vec_piece, preferred_element_type=jnp.float32), None)
    total, unused = lax.scan(step, jnp.zeros((SLAB, RITZ), jnp.float32), (land_blocks, vec_blocks))
    return total * factor[None, :]
```

```python
import math

import jax
import jax.numpy as jnp
from jax import lax
from jax.sharding import PartitionSpec as P

BLOCK = 128


def local(slab, landmarks, codes, exponents, eigvec, ritz):
    total_land = codes.shape[0] * lax.axis_size("lm") * lax.axis_size("sl")
    coeff = 1.0 / math.sqrt(slab.shape[1])
    factor = 1.0 / (ritz * math.sqrt(total_land))
    scale = jnp.exp2(exponents.astype(jnp.float32))
    rows_scale = jnp.repeat(scale, BLOCK)
    basis = (codes.astype(jnp.float32) * rows_scale[:, None]).astype(jnp.bfloat16)
    vectors = jnp.dot(basis, eigvec, preferred_element_type=jnp.float32).astype(jnp.bfloat16)
    land = lax.all_gather(landmarks, "sl", axis=0, tiled=True)
    vec = lax.all_gather(vectors, "sl", axis=0, tiled=True)
    scores = jnp.dot(slab, land.T, preferred_element_type=jnp.float32) * coeff
    affinity = jnp.exp(scores).astype(jnp.bfloat16)
    terms = jnp.dot(affinity, vec, preferred_element_type=jnp.float32)
    summed = lax.psum(terms, "lm")
    return summed * factor[None, :]


def solution(mesh):
    return jax.shard_map(
        local,
        mesh=mesh,
        in_specs=(
            P("sl", None),
            P(("lm", "sl"), None),
            P(("lm", "sl"), None),
            P(("lm", "sl")),
            P(),
            P(),
        ),
        out_specs=P("sl", None),
        check_vma=False,
    )
```

```python
import functools
import math

import jax
import jax.numpy as jnp
from jax import lax
from jax.experimental import pallas as pl
from jax.experimental.pallas import tpu as pltpu
from jax.sharding import PartitionSpec as P

MESH = pl.DeviceIdType.MESH
HALVES = 2
QUARTERS = 4
GROUPS = 8
NT = (((1,), (1,)), ((), ()))
NN = (((1,), (0,)), ((), ()))


def group_of(col, rel, half):
    if rel == 0:
        return col
    if rel == 2:
        return 6 + col
    early = (rel == -1) == (half == 0)
    return (2 if early else 3) + 2 * col


def kernel(
    slab_hbm, land_hbm, codes_ref, exponents_ref, eigvec_ref, out_ref,
    slab, land, vec, acc, swap_out, swap_in, total, rs_out, rs_in, ag_in,
    load_sem, slab_sem, own_send, fwd_send, vec_send, land_recv, vec_recv, swap_sem, rs_send, rs_recv, ag_send, ag_recv,
):
    rows = slab_hbm.shape[0]
    width = land_hbm.shape[0]
    quarter = width // QUARTERS
    n_lm = lax.axis_size("lm")
    chunk = rows // n_lm
    scale = math.log2(math.e) / math.sqrt(slab_hbm.shape[1])

    lm = lax.axis_index("lm")
    sl = lax.axis_index("sl")
    z, x_hi = lm // 2, lm % 2
    y, x_lo, core = sl // 4, (sl // 2) % 2, sl % 2
    x = x_hi * 2 + x_lo
    side = 1 - 2 * core

    def place(dx, dy, flip=0):
        px = lax.rem(x + dx + 4, 4)
        py = lax.rem(y + dy + 4, 4)
        pc = lax.rem(core + flip, 2)
        return (z * 2 + px // 2, py * 4 + lax.rem(px, 2) * 2 + pc)

    def peer(r):
        return (lax.rem(lm + r, n_lm), sl)

    up, down, across, partner = place(0, 1), place(0, -1), place(side, 0), place(0, 0, 1)

    load_slab = pltpu.make_async_copy(slab_hbm, slab.at[0], load_sem.at[0])
    load_land = pltpu.make_async_copy(land_hbm, land.at[0], load_sem.at[1])
    load_slab.start()
    load_land.start()

    barrier = pltpu.get_barrier_semaphore()
    greeted = [place(0, 1), place(0, -1), place(0, 2), partner]
    greeted += [place(d * side, dy) for d in (1, -1) for dy in (0, 1, -1, 2)]
    greeted += [peer(r) for r in range(1, n_lm)]
    for device in greeted:
        pl.semaphore_signal(barrier, inc=1, device_id=device, device_id_type=MESH)

    block = codes_ref.shape[1] // exponents_ref.shape[0]
    for half in range(HALVES):
        grow = jnp.exp2(jnp.full((codes_ref.shape[0], block), exponents_ref[half], jnp.int32).astype(jnp.float32))
        basis = (codes_ref[:, half * block:(half + 1) * block].astype(jnp.float32) * grow).astype(jnp.bfloat16)
        vec[0, half] = lax.dot_general(eigvec_ref[...], basis, NN, preferred_element_type=jnp.float32).astype(jnp.bfloat16)

    pl.semaphore_wait(barrier, len(greeted))

    def remote(src, dst, send, recv, device):
        return pltpu.make_async_remote_copy(
            src_ref=src, dst_ref=dst, send_sem=send, recv_sem=recv, device_id=device, device_id_type=MESH
        )

    sent = []

    def start(copy):
        copy.start()
        sent.append(copy)

    def quarter_of(g, q):
        return land.at[g, pl.ds(q * quarter, quarter)]

    def own(q, g, device, sem):
        start(remote(land_hbm.at[pl.ds(q * quarter, quarter)], quarter_of(g, q), own_send.at[sem], land_recv.at[g, q], device))

    for i in range(QUARTERS):
        own(i, group_of(1, 0, i // 2), across, 3 * i)
        own(i, group_of(0, -1, i // 2), up, 3 * i + 1)
        j = (i + 2) % QUARTERS
        own(j, group_of(0, 1, j // 2), down, 3 * i + 2)

    swap_slab = remote(slab_hbm, slab.at[1], slab_sem.at[0], slab_sem.at[1], partner)
    swap_slab.start()

    n_vec = 0
    for col in (0, 1):
        for rel, dy in ((0, 0), (-1, 1), (1, -1), (2, 2)):
            if col == 0 and rel == 0:
                continue
            for half in range(HALVES):
                g = group_of(col, rel, half)
                start(remote(vec.at[0, half], vec.at[g, half], vec_send.at[n_vec], vec_recv, place(col * side, dy)))
                n_vec += 1

    n_fwd = [0]

    def arrive(g, q):
        remote(quarter_of(g, q), quarter_of(g, q), fwd_send.at[0], land_recv.at[g, q], partner).wait_recv()

    def forward(g, q, to_g, device):
        start(remote(quarter_of(g, q), quarter_of(to_g, q), fwd_send.at[n_fwd[0]], land_recv.at[to_g, q], device))
        n_fwd[0] += 1

    def multiply(g, side_of, first=False):
        scores = lax.dot_general(land[g], slab[side_of], NT, preferred_element_type=jnp.float32)
        affinity = jnp.exp2(scores * scale).astype(jnp.bfloat16)
        coeffs = jnp.concatenate([vec[g, 0], vec[g, 1]], axis=1)
        part = lax.dot_general(coeffs, affinity, NN, preferred_element_type=jnp.float32)
        acc[side_of] = part if first else acc[side_of] + part

    load_slab.wait()
    load_land.wait()
    multiply(0, 0, first=True)
    swap_slab.wait_recv()
    multiply(0, 1, first=True)

    for q0, q1 in ((0, 2), (1, 3)):
        arrive(2, q0)
        forward(2, q0, group_of(1, -1, 0), across)
        forward(2, q0, 6, up)
        arrive(2, q1)
        forward(2, q1, group_of(1, 1, 1), across)
        forward(2, q1, 6, down)
    remote(vec.at[pl.ds(1, GROUPS - 1)], vec.at[pl.ds(1, GROUPS - 1)], fwd_send.at[0], vec_recv, partner).wait_recv()
    for q in range(QUARTERS):
        arrive(1, q)
    for g in (2, 1):
        for s in (0, 1):
            multiply(g, s)

    for q0, q1 in ((0, 2), (1, 3)):
        arrive(3, q1)
        forward(3, q1, group_of(1, -1, 1), across)
        arrive(3, q0)
        forward(3, q0, group_of(1, 1, 0), across)
    for q in (0, 2, 1, 3):
        arrive(4, q)
    forward(4, 1, 7, up)
    forward(4, 3, 7, down)
    for g in (3, 4):
        for s in (0, 1):
            multiply(g, s)

    for q in (0, 2):
        arrive(6, q)
        forward(6, q, 7, across)
    for q in (2, 0, 3, 1):
        arrive(5, q)
    for s in (0, 1):
        multiply(5, s)
    for q in (1, 3):
        arrive(6, q)
    for s in (0, 1):
        multiply(6, s)

    for q in range(QUARTERS):
        arrive(7, q)
    multiply(7, 1)
    swap_out[...] = acc[1].astype(swap_out.dtype)
    swap = remote(swap_out, swap_in, swap_sem.at[0], swap_sem.at[1], partner)
    swap.start()
    multiply(7, 0)
    swap.wait_recv()
    for j in range(n_lm):
        lanes = slice(j * chunk, (j + 1) * chunk)
        piece = acc[0, :, lanes] + swap_in[:, lanes].astype(jnp.float32)
        total[j] = piece
        rs_out[j] = piece.astype(rs_out.dtype)
    for r in (5, 3, 4, 2, 6, 1, 7):
        j = lax.rem(lm + r, n_lm)
        start(remote(rs_out.at[j], rs_in.at[r - 1], rs_send.at[r - 1], rs_recv, peer(r)))
    remote(rs_in, rs_in, fwd_send.at[0], rs_recv, partner).wait_recv()
    piece = total[lm]
    for r in range(n_lm - 1):
        piece = piece + rs_in[r].astype(jnp.float32)
    ag_in[lm] = piece.astype(ag_in.dtype)
    gathered = []
    for r in (5, 3, 4, 2, 6, 1, 7):
        copy = remote(ag_in.at[lm], ag_in.at[lm], ag_send.at[r - 1], ag_recv.at[r - 1], peer(r))
        copy.start()
        gathered.append(copy)
    for copy in gathered:
        copy.wait_recv()
    for j in range(n_lm):
        out_ref[:, j * chunk:(j + 1) * chunk] = ag_in[j].astype(out_ref.dtype)

    for copy in sent + gathered + [swap_slab, swap]:
        copy.wait_send()


def local(slab, landmarks, codes, exponents, eigvec, ritz):
    n_lm, n_sl = lax.axis_size("lm"), lax.axis_size("sl")
    total_land = codes.shape[0] * n_lm * n_sl
    rows, feat = slab.shape
    width = landmarks.shape[0]
    ritz_n = eigvec.shape[1]
    block = codes.shape[0] // exponents.shape[0]
    chunk = rows // n_lm
    wire = jnp.bfloat16
    summed = pl.pallas_call(
        kernel,
        out_shape=jax.ShapeDtypeStruct((ritz_n, rows), jnp.float32),
        in_specs=[
            pl.BlockSpec(memory_space=pl.ANY),
            pl.BlockSpec(memory_space=pl.ANY),
            pl.BlockSpec(memory_space=pltpu.VMEM),
            pl.BlockSpec(memory_space=pltpu.SMEM),
            pl.BlockSpec(memory_space=pltpu.VMEM),
        ],
        out_specs=pl.BlockSpec(memory_space=pltpu.VMEM),
        scratch_shapes=[
            pltpu.VMEM((2, rows, feat), slab.dtype),
            pltpu.VMEM((GROUPS, width, feat), landmarks.dtype),
            pltpu.VMEM((GROUPS, HALVES, ritz_n, block), jnp.bfloat16),
            pltpu.VMEM((2, ritz_n, rows), jnp.float32),
            pltpu.VMEM((ritz_n, rows), wire),
            pltpu.VMEM((ritz_n, rows), wire),
            pltpu.VMEM((n_lm, ritz_n, chunk), jnp.float32),
            pltpu.VMEM((n_lm, ritz_n, chunk), wire),
            pltpu.VMEM((n_lm - 1, ritz_n, chunk), wire),
            pltpu.VMEM((n_lm, ritz_n, chunk), wire),
            pltpu.SemaphoreType.DMA((2,)),
            pltpu.SemaphoreType.DMA((2,)),
            pltpu.SemaphoreType.DMA((3 * QUARTERS,)),
            pltpu.SemaphoreType.DMA((16,)),
            pltpu.SemaphoreType.DMA((14,)),
            pltpu.SemaphoreType.DMA((GROUPS, QUARTERS)),
            pltpu.SemaphoreType.DMA,
            pltpu.SemaphoreType.DMA((2,)),
            pltpu.SemaphoreType.DMA((n_lm - 1,)),
            pltpu.SemaphoreType.DMA,
            pltpu.SemaphoreType.DMA((n_lm - 1,)),
            pltpu.SemaphoreType.DMA((n_lm - 1,)),
        ],
        compiler_params=pltpu.CompilerParams(collective_id=0, has_side_effects=True, vmem_limit_bytes=56 * 2**20),
        name="nystrom",
    )(slab, landmarks, codes.T, exponents, eigvec.T)
    factor = 1.0 / (ritz * math.sqrt(total_land))
    return (summed * factor[:, None]).T


def solution(mesh):
    return jax.shard_map(
        local,
        mesh=mesh,
        in_specs=(
            P("sl", None),
            P(("lm", "sl"), None),
            P(("lm", "sl"), None),
            P(("lm", "sl")),
            P(),
            P(),
        ),
        out_specs=P("sl", None),
        check_vma=False,
    )
```

```python
import functools
import math

import jax
import jax.numpy as jnp
from jax import lax
from jax.experimental import pallas as pl
from jax.experimental.pallas import tpu as pltpu
from jax.sharding import PartitionSpec as P

MESH = pl.DeviceIdType.MESH
HALVES = 2
QUARTERS = 4
GROUPS = 8
NT = (((1,), (1,)), ((), ()))
NN = (((1,), (0,)), ((), ()))


def group_of(col, rel, half):
    if rel == 0:
        return col
    if rel == 2:
        return 6 + col
    early = (rel == -1) == (half == 0)
    return (2 if early else 3) + 2 * col


def kernel(
    slab_hbm, land_hbm, codes_hbm, exponents_hbm, eigvec_hbm, ritz_hbm, out_ref,
    slab, land, vec, acc, swap_out, swap_in, total, rs_out, rs_in, ag_in, codes, exponents, eigvec, ritz,
    load_sem, slab_sem, own_send, fwd_send, vec_send, land_recv, vec_recv, swap_sem, rs_send, rs_recv, ag_send, ag_recv, near,
):
    rows, feat = slab_hbm.shape
    width = land_hbm.shape[0]
    quarter = width // QUARTERS
    n_lm, n_sl = lax.axis_size("lm"), lax.axis_size("sl")
    chunk = rows // n_lm
    scale = math.log2(math.e) / math.sqrt(feat)

    lm = lax.axis_index("lm")
    sl = lax.axis_index("sl")
    z, x_hi = lm // 2, lm % 2
    y, x_lo, core = sl // 4, (sl // 2) % 2, sl % 2
    x = x_hi * 2 + x_lo
    side = 1 - 2 * core

    def place(dx, dy, dz=0, flip=0):
        px = lax.rem(x + dx + 4, 4)
        py = lax.rem(y + dy + 4, 4)
        pz = lax.rem(z + dz + 4, 4)
        pc = lax.rem(core + flip, 2)
        return (pz * 2 + px // 2, py * 4 + lax.rem(px, 2) * 2 + pc)

    def peer(r):
        return (lax.rem(lm + r, n_lm), sl)

    up, down, across, partner = place(0, 1), place(0, -1), place(side, 0), place(0, 0, 0, 1)
    ring = [across, place(-side, 0), place(0, 0, 1), place(0, 0, -1)]

    def greet(semaphore, devices):
        for device in devices:
            pl.semaphore_signal(semaphore, inc=1, device_id=device, device_id_type=MESH)

    barrier = pltpu.get_barrier_semaphore()
    greeted = ring + [up, down, partner]
    greet(barrier, greeted)
    loads = [
        pltpu.make_async_copy(src, dst, load_sem.at[i])
        for i, (src, dst) in enumerate((
            (codes_hbm, codes), (eigvec_hbm, eigvec), (exponents_hbm, exponents), (ritz_hbm, ritz),
            (land_hbm, land.at[0]), (slab_hbm, slab.at[pl.ds(0, rows)]),
        ))
    ]
    for load in loads:
        load.start()
    pl.semaphore_wait(barrier, len(greeted))

    def remote(src, dst, send, recv, device):
        return pltpu.make_async_remote_copy(
            src_ref=src, dst_ref=dst, send_sem=send, recv_sem=recv, device_id=device, device_id_type=MESH
        )

    sent = []

    def start(copy):
        copy.start()
        sent.append(copy)

    def quarter_of(g, q):
        return land.at[g, pl.ds(q * quarter, quarter)]

    def own(i):
        for k, (col, rel, device) in enumerate(((1, 0, across), (0, -1, up), (0, 1, down))):
            q = (i + 2) % QUARTERS if rel == 1 else i
            g = group_of(col, rel, q // 2)
            src = land_hbm.at[pl.ds(q * quarter, quarter)]
            start(remote(src, quarter_of(g, q), own_send.at[3 * i + k], land_recv.at[g, q], device))

    n_vec = [0]

    def send_vec(g, half, to_g, device):
        start(remote(vec.at[g, half], vec.at[to_g, half], vec_send.at[n_vec[0]], vec_recv.at[to_g, half], device))
        n_vec[0] += 1

    def arrive_vec(g, half):
        remote(vec.at[g, half], vec.at[g, half], vec_send.at[0], vec_recv.at[g, half], partner).wait_recv()

    own(0)
    swap_slab = remote(slab_hbm, slab.at[pl.ds(rows, rows)], slab_sem.at[0], slab_sem.at[1], partner)
    swap_slab.start()
    for load in loads[:4]:
        load.wait()
    block = codes.shape[1] // HALVES
    for half in range(HALVES):
        grow = jnp.exp2(jnp.full((codes.shape[0], block), exponents[half], jnp.int32).astype(jnp.float32))
        basis = (codes[:, half * block:(half + 1) * block].astype(jnp.float32) * grow).astype(jnp.bfloat16)
        vec[0, half] = lax.dot_general(eigvec[...], basis, NN, preferred_element_type=jnp.float32).astype(jnp.bfloat16)
    for half in range(HALVES):
        for col, rel, device in ((0, -1, up), (0, 1, down), (1, 0, across)):
            send_vec(0, half, group_of(col, rel, half), device)
    for i in range(1, QUARTERS):
        own(i)
    greet(near.at[0], ring)

    n_fwd = [0]

    def arrive(g, q):
        remote(quarter_of(g, q), quarter_of(g, q), fwd_send.at[0], land_recv.at[g, q], partner).wait_recv()

    def forward(g, q, to_g, device):
        start(remote(quarter_of(g, q), quarter_of(to_g, q), fwd_send.at[n_fwd[0]], land_recv.at[to_g, q], device))
        n_fwd[0] += 1

    def multiply(g, n, lo, hi, first=False):
        part_of = slice(lo * rows, hi * rows)
        left = land[g:g + n].reshape(n * width, feat)
        scores = lax.dot_general(left, slab[part_of], NT, preferred_element_type=jnp.float32)
        affinity = jnp.exp2(scores * scale).astype(jnp.bfloat16)
        coeffs = jnp.concatenate([vec[g + i, half] for i in range(n) for half in range(HALVES)], axis=1)
        part = lax.dot_general(coeffs, affinity, NN, preferred_element_type=jnp.float32)
        acc[:, part_of] = part if first else acc[:, part_of] + part

    for load in loads[4:]:
        load.wait()
    multiply(0, 1, 0, 1, first=True)

    for g in (2, 3):
        for half in range(HALVES):
            arrive_vec(g, half)
            send_vec(g, half, g + 2, across)
            if g == 2:
                send_vec(g, half, 6, (up, down)[half])

    def step2(q0, q1):
        arrive(2, q0)
        forward(2, q0, 4, across)
        forward(2, q0, 6, up)
        arrive(2, q1)
        forward(2, q1, 4, across)
        forward(2, q1, 6, down)

    step2(0, 2)
    pl.semaphore_wait(near.at[0], len(ring))
    greet(near.at[1], ring)
    swap_slab.wait_recv()
    multiply(0, 1, 1, 2, first=True)
    step2(1, 3)
    for half in range(HALVES):
        arrive_vec(1, half)
    for q in range(QUARTERS):
        arrive(1, q)
    multiply(1, 2, 0, 2)

    for q0, q1 in ((0, 2), (1, 3)):
        arrive(3, q1)
        forward(3, q1, 5, across)
        arrive(3, q0)
        forward(3, q0, 5, across)
    pl.semaphore_wait(near.at[1], len(ring))
    greet(near.at[2], ring)
    for q in (0, 2, 1, 3):
        arrive(4, q)
    forward(4, 1, 7, up)
    forward(4, 3, 7, down)
    for half in range(HALVES):
        arrive_vec(6, half)
        send_vec(6, half, 7, across)
        arrive_vec(4, half)
    multiply(3, 2, 0, 2)

    for q in (0, 2):
        arrive(6, q)
        forward(6, q, 7, across)
    for half in range(HALVES):
        arrive_vec(5, half)
    for q in (2, 0, 3, 1):
        arrive(5, q)
    for q in (1, 3):
        arrive(6, q)
    multiply(5, 2, 0, 2)

    factor_row = 1.0 / (ritz[...] * math.sqrt(width * n_lm * n_sl))
    n_ritz = factor_row.shape[1]
    diagonal = lax.broadcasted_iota(jnp.int32, (n_ritz, n_ritz), 0) == lax.broadcasted_iota(jnp.int32, (n_ritz, n_ritz), 1)
    factor = jnp.sum(jnp.where(diagonal, factor_row, 0.0), axis=1, keepdims=True)

    for half in range(HALVES):
        arrive_vec(7, half)
    for q in (0, 2, 1, 3):
        arrive(7, q)
    multiply(7, 1, 1, 2)
    swap_out[...] = acc[:, rows:]
    swap = remote(swap_out, swap_in, swap_sem.at[0], swap_sem.at[1], partner)
    swap.start()
    multiply(7, 1, 0, 1)
    pl.semaphore_wait(near.at[2], len(ring))
    swap.wait_recv()
    for j in range(n_lm):
        lanes = slice(j * chunk, (j + 1) * chunk)
        piece = acc[:, lanes] + swap_in[:, lanes]
        total[j] = piece
        rs_out[j] = piece.astype(rs_out.dtype)
    for r in (5, 3, 4, 2, 6, 1, 7):
        j = lax.rem(lm + r, n_lm)
        start(remote(rs_out.at[j], rs_in.at[r - 1], rs_send.at[r - 1], rs_recv, peer(r)))
    remote(rs_in, rs_in, fwd_send.at[0], rs_recv, partner).wait_recv()
    piece = total[lm]
    for r in range(n_lm - 1):
        piece = piece + rs_in[r].astype(jnp.float32)
    ag_in[lm] = (piece * factor).astype(ag_in.dtype)
    gathered = []
    for r in (5, 3, 4, 2, 6, 1, 7):
        copy = remote(ag_in.at[lm], ag_in.at[lm], ag_send.at[r - 1], ag_recv.at[r - 1], peer(r))
        copy.start()
        gathered.append(copy)
    for copy in gathered:
        copy.wait_recv()
    for j in range(n_lm):
        out_ref[:, j * chunk:(j + 1) * chunk] = ag_in[j].astype(out_ref.dtype)

    for copy in sent + gathered + [swap_slab, swap]:
        copy.wait_send()


def local(slab, landmarks, codes, exponents, eigvec, ritz):
    n_lm = lax.axis_size("lm")
    rows, feat = slab.shape
    width = landmarks.shape[0]
    n_ritz = eigvec.shape[1]
    block = codes.shape[0] // exponents.shape[0]
    chunk = rows // n_lm
    wire = jnp.bfloat16
    dma = pltpu.SemaphoreType.DMA
    extended = pl.pallas_call(
        kernel,
        out_shape=jax.ShapeDtypeStruct((n_ritz, rows), jnp.float32),
        in_specs=[pl.BlockSpec(memory_space=pl.ANY)] * 6,
        out_specs=pl.BlockSpec(memory_space=pltpu.VMEM),
        scratch_shapes=[
            pltpu.VMEM((2 * rows, feat), slab.dtype),
            pltpu.VMEM((GROUPS, width, feat), landmarks.dtype),
            pltpu.VMEM((GROUPS, HALVES, n_ritz, block), jnp.bfloat16),
            pltpu.VMEM((n_ritz, 2 * rows), jnp.float32),
            pltpu.VMEM((n_ritz, rows), jnp.float32),
            pltpu.VMEM((n_ritz, rows), jnp.float32),
            pltpu.VMEM((n_lm, n_ritz, chunk), jnp.float32),
            pltpu.VMEM((n_lm, n_ritz, chunk), wire),
            pltpu.VMEM((n_lm - 1, n_ritz, chunk), wire),
            pltpu.VMEM((n_lm, n_ritz, chunk), wire),
            pltpu.VMEM(codes.shape[::-1], codes.dtype),
            pltpu.SMEM(exponents.shape, exponents.dtype),
            pltpu.VMEM(eigvec.shape[::-1], eigvec.dtype),
            pltpu.VMEM((1, n_ritz), ritz.dtype),
            dma((6,)),
            dma((2,)),
            dma((3 * QUARTERS,)),
            dma((16,)),
            dma((14,)),
            dma((GROUPS, QUARTERS)),
            dma((GROUPS, HALVES)),
            dma((2,)),
            dma((n_lm - 1,)),
            dma,
            dma((n_lm - 1,)),
            dma((n_lm - 1,)),
            pltpu.SemaphoreType.REGULAR((3,)),
        ],
        compiler_params=pltpu.CompilerParams(collective_id=0, has_side_effects=True, vmem_limit_bytes=56 * 2**20),
        name="nystrom",
    )(slab, landmarks, codes.T, exponents, eigvec.T, ritz.reshape(1, n_ritz))
    return extended.T


def solution(mesh):
    return jax.shard_map(
        local,
        mesh=mesh,
        in_specs=(
            P("sl", None),
            P(("lm", "sl"), None),
            P(("lm", "sl"), None),
            P(("lm", "sl")),
            P(),
            P(),
        ),
        out_specs=P("sl", None),
        check_vma=False,
    )
```

```python
import functools
import math

import jax
import jax.numpy as jnp
from jax import lax
from jax.experimental import pallas as pl
from jax.experimental.pallas import tpu as pltpu
from jax.sharding import PartitionSpec as P

MESH = pl.DeviceIdType.MESH
HALVES = 2
QUARTERS = 4
GROUPS = 8
NT = (((1,), (1,)), ((), ()))
NN = (((1,), (0,)), ((), ()))


def group_of(col, rel, half):
    if rel == 0:
        return col
    if rel == 2:
        return 6 + col
    early = (rel == -1) == (half == 0)
    return (2 if early else 3) + 2 * col


def kernel(
    slab_hbm, land_hbm, codes_hbm, exponents_hbm, eigvec_hbm, ritz_hbm, out_hbm,
    slab, land, vec, acc, swap_out, swap_in, total, rs_out, rs_in, ag_in, out, codes, exponents, eigvec, ritz,
    load_sem, slab_sem, own_send, fwd_send, vec_send, land_recv, vec_recv, swap_sem, rs_send, rs_recv, ag_send, ag_recv, near, out_sem,
):
    rows, feat = slab_hbm.shape
    width = land_hbm.shape[0]
    quarter = width // QUARTERS
    n_lm, n_sl = lax.axis_size("lm"), lax.axis_size("sl")
    chunk = rows // n_lm
    scale = math.log2(math.e) / math.sqrt(feat)

    lm = lax.axis_index("lm")
    sl = lax.axis_index("sl")
    z, x_hi = lm // 2, lm % 2
    y, x_lo, core = sl // 4, (sl // 2) % 2, sl % 2
    x = x_hi * 2 + x_lo
    side = 1 - 2 * core

    def place(dx, dy, dz=0, flip=0):
        px = lax.rem(x + dx + 4, 4)
        py = lax.rem(y + dy + 4, 4)
        pz = lax.rem(z + dz + 4, 4)
        pc = lax.rem(core + flip, 2)
        return (pz * 2 + px // 2, py * 4 + lax.rem(px, 2) * 2 + pc)

    def peer(r):
        return (lax.rem(lm + r, n_lm), sl)

    up, down, across, partner = place(0, 1), place(0, -1), place(side, 0), place(0, 0, 0, 1)
    ring = [across, place(-side, 0), place(0, 0, 1), place(0, 0, -1)]

    def greet(semaphore, devices):
        for device in devices:
            pl.semaphore_signal(semaphore, inc=1, device_id=device, device_id_type=MESH)

    barrier = pltpu.get_barrier_semaphore()
    greeted = ring + [up, down, partner]
    greet(barrier, greeted)
    loads = [
        pltpu.make_async_copy(src, dst, load_sem.at[i])
        for i, (src, dst) in enumerate((
            (codes_hbm, codes), (eigvec_hbm, eigvec), (exponents_hbm, exponents), (ritz_hbm, ritz),
            (land_hbm, land.at[0]), (slab_hbm, slab.at[pl.ds(0, rows)]),
        ))
    ]
    for load in loads:
        load.start()
    pl.semaphore_wait(barrier, len(greeted))

    def remote(src, dst, send, recv, device):
        return pltpu.make_async_remote_copy(
            src_ref=src, dst_ref=dst, send_sem=send, recv_sem=recv, device_id=device, device_id_type=MESH
        )

    sent = []

    def start(copy):
        copy.start()
        sent.append(copy)

    def quarter_of(g, q):
        return land.at[g, pl.ds(q * quarter, quarter)]

    def own(i):
        for k, (col, rel, device) in enumerate(((1, 0, across), (0, -1, up), (0, 1, down))):
            q = (i + 2) % QUARTERS if rel == 1 else i
            g = group_of(col, rel, q // 2)
            src = land_hbm.at[pl.ds(q * quarter, quarter)]
            start(remote(src, quarter_of(g, q), own_send.at[3 * i + k], land_recv.at[g, q], device))

    n_vec = [0]

    def send_vec(g, half, to_g, device):
        start(remote(vec.at[g, half], vec.at[to_g, half], vec_send.at[n_vec[0]], vec_recv.at[to_g, half], device))
        n_vec[0] += 1

    def arrive_vec(g, half):
        remote(vec.at[g, half], vec.at[g, half], vec_send.at[0], vec_recv.at[g, half], partner).wait_recv()

    own(0)
    swap_slab = remote(slab_hbm, slab.at[pl.ds(rows, rows)], slab_sem.at[0], slab_sem.at[1], partner)
    swap_slab.start()
    for load in loads[:4]:
        load.wait()
    block = codes.shape[1] // HALVES
    for half in range(HALVES):
        grow = jnp.exp2(jnp.full((codes.shape[0], block), exponents[half], jnp.int32).astype(jnp.float32))
        basis = (codes[:, half * block:(half + 1) * block].astype(jnp.float32) * grow).astype(jnp.bfloat16)
        vec[0, half] = lax.dot_general(eigvec[...], basis, NN, preferred_element_type=jnp.float32).astype(jnp.bfloat16)
    for half in range(HALVES):
        for col, rel, device in ((0, -1, up), (0, 1, down), (1, 0, across)):
            send_vec(0, half, group_of(col, rel, half), device)
    for i in range(1, QUARTERS):
        own(i)
    greet(near.at[0], ring)

    n_fwd = [0]

    def arrive(g, q):
        remote(quarter_of(g, q), quarter_of(g, q), fwd_send.at[0], land_recv.at[g, q], partner).wait_recv()

    def forward(g, q, to_g, device):
        start(remote(quarter_of(g, q), quarter_of(to_g, q), fwd_send.at[n_fwd[0]], land_recv.at[to_g, q], device))
        n_fwd[0] += 1

    def multiply(g, n, lo, hi, first=False):
        part_of = slice(lo * rows, hi * rows)
        left = land[g:g + n].reshape(n * width, feat)
        scores = lax.dot_general(left, slab[part_of], NT, preferred_element_type=jnp.float32)
        affinity = jnp.exp2(scores * scale).astype(jnp.bfloat16)
        coeffs = jnp.concatenate([vec[g + i, half] for i in range(n) for half in range(HALVES)], axis=1)
        part = lax.dot_general(coeffs, affinity, NN, preferred_element_type=jnp.float32)
        acc[:, part_of] = part if first else acc[:, part_of] + part

    for load in loads[4:]:
        load.wait()
    multiply(0, 1, 0, 1, first=True)

    for g in (2, 3):
        for half in range(HALVES):
            arrive_vec(g, half)
            send_vec(g, half, g + 2, across)
            if g == 2:
                send_vec(g, half, 6, (up, down)[half])

    def step2(q0, q1):
        arrive(2, q0)
        forward(2, q0, 4, across)
        forward(2, q0, 6, up)
        arrive(2, q1)
        forward(2, q1, 4, across)
        forward(2, q1, 6, down)

    step2(0, 2)
    pl.semaphore_wait(near.at[0], len(ring))
    greet(near.at[1], ring)
    swap_slab.wait_recv()
    multiply(0, 1, 1, 2, first=True)
    step2(1, 3)
    for half in range(HALVES):
        arrive_vec(1, half)
    for q in range(QUARTERS):
        arrive(1, q)
    multiply(1, 2, 0, 2)

    for q0, q1 in ((0, 2), (1, 3)):
        arrive(3, q1)
        forward(3, q1, 5, across)
        arrive(3, q0)
        forward(3, q0, 5, across)
    pl.semaphore_wait(near.at[1], len(ring))
    greet(near.at[2], ring)
    for q in (0, 2, 1, 3):
        arrive(4, q)
    forward(4, 1, 7, up)
    forward(4, 3, 7, down)
    for half in range(HALVES):
        arrive_vec(6, half)
        send_vec(6, half, 7, across)
        arrive_vec(4, half)
    multiply(3, 2, 0, 2)

    for q in (0, 2):
        arrive(6, q)
        forward(6, q, 7, across)
    for half in range(HALVES):
        arrive_vec(5, half)
    for q in (2, 0, 3, 1):
        arrive(5, q)
    for q in (1, 3):
        arrive(6, q)
    multiply(5, 2, 0, 2)

    factor_row = 1.0 / (ritz[...] * math.sqrt(width * n_lm * n_sl))
    n_ritz = factor_row.shape[1]
    diagonal = lax.broadcasted_iota(jnp.int32, (n_ritz, n_ritz), 0) == lax.broadcasted_iota(jnp.int32, (n_ritz, n_ritz), 1)
    factor = jnp.sum(jnp.where(diagonal, factor_row, 0.0), axis=1, keepdims=True)

    for half in range(HALVES):
        arrive_vec(7, half)
    for q in (0, 2, 1, 3):
        arrive(7, q)
    multiply(7, 1, 1, 2)
    swap_out[...] = acc[:, rows:]
    swap = remote(swap_out, swap_in, swap_sem.at[0], swap_sem.at[1], partner)
    swap.start()
    multiply(7, 1, 0, 1)
    pl.semaphore_wait(near.at[2], len(ring))
    swap.wait_recv()
    for j in range(n_lm):
        lanes = slice(j * chunk, (j + 1) * chunk)
        piece = acc[:, lanes] + swap_in[:, lanes]
        total[j] = piece
        rs_out[j] = piece.astype(rs_out.dtype)
    for r in (5, 3, 4, 2, 6, 1, 7):
        j = lax.rem(lm + r, n_lm)
        start(remote(rs_out.at[j], rs_in.at[r - 1], rs_send.at[r - 1], rs_recv, peer(r)))
    remote(rs_in, rs_in, fwd_send.at[0], rs_recv, partner).wait_recv()
    piece = total[lm]
    for r in range(n_lm - 1):
        piece = piece + rs_in[r].astype(jnp.float32)
    ag_in[lm] = (piece * factor).astype(ag_in.dtype)
    gathered, written = {}, []
    for r in (5, 3, 4, 2, 6, 1, 7):
        copy = remote(ag_in.at[lm], ag_in.at[lm], ag_send.at[r - 1], ag_recv.at[r - 1], peer(r))
        copy.start()
        gathered[r] = copy

    for r in (0, 2, 6, 4, 1, 7, 3, 5):
        if r:
            gathered[r].wait_recv()
        j = lax.rem(lm + n_lm - r, n_lm)
        out[j] = ag_in[j].astype(out.dtype)
        written.append(pltpu.make_async_copy(out.at[j], out_hbm.at[:, pl.ds(pl.multiple_of(j * chunk, chunk), chunk)], out_sem.at[r]))
        written[-1].start()

    for copy in sent + list(gathered.values()) + [swap_slab, swap]:
        copy.wait_send()
    for copy in written:
        copy.wait()


def local(slab, landmarks, codes, exponents, eigvec, ritz):
    n_lm = lax.axis_size("lm")
    rows, feat = slab.shape
    width = landmarks.shape[0]
    n_ritz = eigvec.shape[1]
    block = codes.shape[0] // exponents.shape[0]
    chunk = rows // n_lm
    wire = jnp.bfloat16
    dma = pltpu.SemaphoreType.DMA
    extended = pl.pallas_call(
        kernel,
        out_shape=jax.ShapeDtypeStruct((n_ritz, rows), jnp.float32),
        in_specs=[pl.BlockSpec(memory_space=pl.ANY)] * 6,
        out_specs=pl.BlockSpec(memory_space=pl.ANY),
        scratch_shapes=[
            pltpu.VMEM((2 * rows, feat), slab.dtype),
            pltpu.VMEM((GROUPS, width, feat), landmarks.dtype),
            pltpu.VMEM((GROUPS, HALVES, n_ritz, block), jnp.bfloat16),
            pltpu.VMEM((n_ritz, 2 * rows), jnp.float32),
            pltpu.VMEM((n_ritz, rows), jnp.float32),
            pltpu.VMEM((n_ritz, rows), jnp.float32),
            pltpu.VMEM((n_lm, n_ritz, chunk), jnp.float32),
            pltpu.VMEM((n_lm, n_ritz, chunk), wire),
            pltpu.VMEM((n_lm - 1, n_ritz, chunk), wire),
            pltpu.VMEM((n_lm, n_ritz, chunk), wire),
            pltpu.VMEM((n_lm, n_ritz, chunk), jnp.float32),
            pltpu.VMEM(codes.shape[::-1], codes.dtype),
            pltpu.SMEM(exponents.shape, exponents.dtype),
            pltpu.VMEM(eigvec.shape[::-1], eigvec.dtype),
            pltpu.VMEM((1, n_ritz), ritz.dtype),
            dma((6,)),
            dma((2,)),
            dma((3 * QUARTERS,)),
            dma((16,)),
            dma((14,)),
            dma((GROUPS, QUARTERS)),
            dma((GROUPS, HALVES)),
            dma((2,)),
            dma((n_lm - 1,)),
            dma,
            dma((n_lm - 1,)),
            dma((n_lm - 1,)),
            pltpu.SemaphoreType.REGULAR((3,)),
            dma((n_lm,)),
        ],
        compiler_params=pltpu.CompilerParams(collective_id=0, has_side_effects=True, vmem_limit_bytes=56 * 2**20),
        name="nystrom",
    )(slab, landmarks, codes.T, exponents, eigvec.T, ritz.reshape(1, n_ritz))
    return extended.T


def solution(mesh):
    return jax.shard_map(
        local,
        mesh=mesh,
        in_specs=(
            P("sl", None),
            P(("lm", "sl"), None),
            P(("lm", "sl"), None),
            P(("lm", "sl")),
            P(),
            P(),
        ),
        out_specs=P("sl", None),
        check_vma=False,
    )
```

```python
import functools
import math

import jax
import jax.numpy as jnp
from jax import lax
from jax.experimental import pallas as pl
from jax.experimental.pallas import tpu as pltpu
from jax.sharding import PartitionSpec as P

MESH = pl.DeviceIdType.MESH
HALVES = 2
QUARTERS = 4
GROUPS = 8
NT = (((1,), (1,)), ((), ()))
NN = (((1,), (0,)), ((), ()))


def group_of(col, rel, half):
    if rel == 0:
        return col
    if rel == 2:
        return 6 + col
    early = (rel == -1) == (half == 0)
    return (2 if early else 3) + 2 * col


def kernel(
    slab_hbm, land_hbm, codes_hbm, exponents_hbm, eigvec_hbm, ritz_hbm, out_ref,
    slab, land, vec, acc, swap_out, swap_in, rs_out, rs_in, ag_in, codes, exponents, eigvec, ritz,
    load_sem, slab_sem, own_send, fwd_send, vec_send, land_recv, vec_recv, swap_sem, rs_send, rs_recv, ag_send, ag_recv, near,
):
    rows, feat = slab_hbm.shape
    width = land_hbm.shape[0]
    quarter = width // QUARTERS
    n_lm, n_sl = lax.axis_size("lm"), lax.axis_size("sl")
    chunk = rows // n_lm
    scale = math.log2(math.e) / math.sqrt(feat)

    lm = lax.axis_index("lm")
    sl = lax.axis_index("sl")
    z, x_hi = lm // 2, lm % 2
    y, x_lo, core = sl // 4, (sl // 2) % 2, sl % 2
    x = x_hi * 2 + x_lo
    side = 1 - 2 * core

    def place(dx, dy, dz=0, flip=0):
        px = lax.rem(x + dx + 4, 4)
        py = lax.rem(y + dy + 4, 4)
        pz = lax.rem(z + dz + 4, 4)
        pc = lax.rem(core + flip, 2)
        return (pz * 2 + px // 2, py * 4 + lax.rem(px, 2) * 2 + pc)

    def peer(r):
        return (lax.rem(lm + r, n_lm), sl)

    up, down, across, partner = place(0, 1), place(0, -1), place(side, 0), place(0, 0, 0, 1)
    ring = [across, place(-side, 0), place(0, 0, 1), place(0, 0, -1)]

    def greet(semaphore, devices):
        for device in devices:
            pl.semaphore_signal(semaphore, inc=1, device_id=device, device_id_type=MESH)

    barrier = pltpu.get_barrier_semaphore()
    greeted = ring + [up, down, partner]
    greet(barrier, greeted)
    loads = [
        pltpu.make_async_copy(src, dst, load_sem.at[i])
        for i, (src, dst) in enumerate((
            (codes_hbm, codes), (eigvec_hbm, eigvec), (exponents_hbm, exponents), (ritz_hbm, ritz),
            (land_hbm, land.at[0]), (slab_hbm, slab.at[pl.ds(0, rows)]),
        ))
    ]
    for load in loads:
        load.start()
    pl.semaphore_wait(barrier, len(greeted))

    def remote(src, dst, send, recv, device):
        return pltpu.make_async_remote_copy(
            src_ref=src, dst_ref=dst, send_sem=send, recv_sem=recv, device_id=device, device_id_type=MESH
        )

    sent = []

    def start(copy):
        copy.start()
        sent.append(copy)

    def quarter_of(g, q):
        return land.at[g, pl.ds(q * quarter, quarter)]

    def own(i):
        for k, (col, rel, device) in enumerate(((1, 0, across), (0, -1, up), (0, 1, down))):
            q = (i + 2) % QUARTERS if rel == 1 else i
            g = group_of(col, rel, q // 2)
            src = land_hbm.at[pl.ds(q * quarter, quarter)]
            start(remote(src, quarter_of(g, q), own_send.at[3 * i + k], land_recv.at[g, q], device))

    n_vec = [0]

    def send_vec(g, half, to_g, device):
        start(remote(vec.at[g, half], vec.at[to_g, half], vec_send.at[n_vec[0]], vec_recv.at[to_g, half], device))
        n_vec[0] += 1

    def arrive_vec(g, half):
        remote(vec.at[g, half], vec.at[g, half], vec_send.at[0], vec_recv.at[g, half], partner).wait_recv()

    own(0)
    swap_slab = remote(slab_hbm, slab.at[pl.ds(rows, rows)], slab_sem.at[0], slab_sem.at[1], partner)
    swap_slab.start()
    for load in loads[:4]:
        load.wait()
    block = codes.shape[1] // HALVES
    for half in range(HALVES):
        grow = jnp.exp2(jnp.full((codes.shape[0], block), exponents[half], jnp.int32).astype(jnp.float32))
        basis = (codes[:, half * block:(half + 1) * block].astype(jnp.float32) * grow).astype(jnp.bfloat16)
        vec[0, half] = lax.dot_general(eigvec[...], basis, NN, preferred_element_type=jnp.float32).astype(jnp.bfloat16)
    for half in range(HALVES):
        for col, rel, device in ((0, -1, up), (0, 1, down), (1, 0, across)):
            send_vec(0, half, group_of(col, rel, half), device)
    for i in range(1, QUARTERS):
        own(i)
    greet(near.at[0], ring)

    n_fwd = [0]

    def arrive(g, q):
        remote(quarter_of(g, q), quarter_of(g, q), fwd_send.at[0], land_recv.at[g, q], partner).wait_recv()

    def forward(g, q, to_g, device):
        start(remote(quarter_of(g, q), quarter_of(to_g, q), fwd_send.at[n_fwd[0]], land_recv.at[to_g, q], device))
        n_fwd[0] += 1

    def multiply(g, n, lo, hi, first=False):
        part_of = slice(lo * rows, hi * rows)
        left = land[g:g + n].reshape(n * width, feat)
        scores = lax.dot_general(left, slab[part_of], NT, preferred_element_type=jnp.float32)
        affinity = jnp.exp2(scores * scale).astype(jnp.bfloat16)
        coeffs = jnp.concatenate([vec[g + i, half] for i in range(n) for half in range(HALVES)], axis=1)
        part = lax.dot_general(coeffs, affinity, NN, preferred_element_type=jnp.float32)
        acc[:, part_of] = part if first else acc[:, part_of] + part

    for load in loads[4:]:
        load.wait()
    multiply(0, 1, 0, 1, first=True)

    for g in (2, 3):
        for half in range(HALVES):
            arrive_vec(g, half)
            send_vec(g, half, g + 2, across)
            if g == 2:
                send_vec(g, half, 6, (up, down)[half])

    def step2(q0, q1):
        arrive(2, q0)
        forward(2, q0, 4, across)
        forward(2, q0, 6, up)
        arrive(2, q1)
        forward(2, q1, 4, across)
        forward(2, q1, 6, down)

    step2(0, 2)
    pl.semaphore_wait(near.at[0], len(ring))
    greet(near.at[1], ring)
    swap_slab.wait_recv()
    multiply(0, 1, 1, 2, first=True)
    step2(1, 3)
    for half in range(HALVES):
        arrive_vec(1, half)
    for q in range(QUARTERS):
        arrive(1, q)
    multiply(1, 2, 0, 2)

    for q0, q1 in ((0, 2), (1, 3)):
        arrive(3, q1)
        forward(3, q1, 5, across)
        arrive(3, q0)
        forward(3, q0, 5, across)
    pl.semaphore_wait(near.at[1], len(ring))
    greet(near.at[2], ring)
    for q in (0, 2, 1, 3):
        arrive(4, q)
    forward(4, 1, 7, up)
    forward(4, 3, 7, down)
    for half in range(HALVES):
        arrive_vec(6, half)
        send_vec(6, half, 7, across)
        arrive_vec(4, half)
    multiply(3, 2, 0, 2)

    for q in (0, 2):
        arrive(6, q)
        forward(6, q, 7, across)
    for half in range(HALVES):
        arrive_vec(5, half)
    for q in (2, 0, 3, 1):
        arrive(5, q)
    for q in (1, 3):
        arrive(6, q)
    multiply(5, 2, 0, 2)

    factor_row = 1.0 / (ritz[...] * math.sqrt(width * n_lm * n_sl))
    n_ritz = factor_row.shape[1]
    diagonal = lax.broadcasted_iota(jnp.int32, (n_ritz, n_ritz), 0) == lax.broadcasted_iota(jnp.int32, (n_ritz, n_ritz), 1)
    factor = jnp.sum(jnp.where(diagonal, factor_row, 0.0), axis=1, keepdims=True)

    for half in range(HALVES):
        arrive_vec(7, half)
    for q in (0, 2, 1, 3):
        arrive(7, q)
    multiply(7, 1, 1, 2)
    swap_out[...] = acc[:, rows:].astype(swap_out.dtype)
    swap = remote(swap_out, swap_in, swap_sem.at[0], swap_sem.at[1], partner)
    swap.start()
    multiply(7, 1, 0, 1)
    pl.semaphore_wait(near.at[2], len(ring))
    swap.wait_recv()
    for r in (5, 3, 4, 2, 6, 1, 7, 0):
        j = lax.rem(lm + r, n_lm)
        lanes = pl.ds(pl.multiple_of(j * chunk, chunk), chunk)
        piece = acc[:, lanes] + swap_in[:, lanes].astype(jnp.float32)
        if r:
            rs_out[j] = piece.astype(rs_out.dtype)
            start(remote(rs_out.at[j], rs_in.at[r - 1], rs_send.at[r - 1], rs_recv, peer(r)))
    remote(rs_in, rs_in, fwd_send.at[0], rs_recv, partner).wait_recv()
    for r in range(n_lm - 1):
        piece = piece + rs_in[r].astype(jnp.float32)
    ag_in[lm] = (piece * factor).astype(ag_in.dtype)
    gathered = []
    for r in (5, 3, 4, 2, 6, 1, 7):
        copy = remote(ag_in.at[lm], ag_in.at[lm], ag_send.at[r - 1], ag_recv.at[r - 1], peer(r))
        copy.start()
        gathered.append(copy)
    for copy in gathered:
        copy.wait_recv()
    for j in range(n_lm):
        out_ref[:, j * chunk:(j + 1) * chunk] = ag_in[j].astype(out_ref.dtype)

    for copy in sent + gathered + [swap_slab, swap]:
        copy.wait_send()


def local(slab, landmarks, codes, exponents, eigvec, ritz):
    n_lm = lax.axis_size("lm")
    rows, feat = slab.shape
    width = landmarks.shape[0]
    n_ritz = eigvec.shape[1]
    block = codes.shape[0] // exponents.shape[0]
    chunk = rows // n_lm
    wire = jnp.bfloat16
    dma = pltpu.SemaphoreType.DMA
    extended = pl.pallas_call(
        kernel,
        out_shape=jax.ShapeDtypeStruct((n_ritz, rows), jnp.float32),
        in_specs=[pl.BlockSpec(memory_space=pl.ANY)] * 6,
        out_specs=pl.BlockSpec(memory_space=pltpu.VMEM),
        scratch_shapes=[
            pltpu.VMEM((2 * rows, feat), slab.dtype),
            pltpu.VMEM((GROUPS, width, feat), landmarks.dtype),
            pltpu.VMEM((GROUPS, HALVES, n_ritz, block), jnp.bfloat16),
            pltpu.VMEM((n_ritz, 2 * rows), jnp.float32),
            pltpu.VMEM((n_ritz, rows), wire),
            pltpu.VMEM((n_ritz, rows), wire),
            pltpu.VMEM((n_lm, n_ritz, chunk), wire),
            pltpu.VMEM((n_lm - 1, n_ritz, chunk), wire),
            pltpu.VMEM((n_lm, n_ritz, chunk), wire),
            pltpu.VMEM(codes.shape[::-1], codes.dtype),
            pltpu.SMEM(exponents.shape, exponents.dtype),
            pltpu.VMEM(eigvec.shape[::-1], eigvec.dtype),
            pltpu.VMEM((1, n_ritz), ritz.dtype),
            dma((6,)),
            dma((2,)),
            dma((3 * QUARTERS,)),
            dma((16,)),
            dma((14,)),
            dma((GROUPS, QUARTERS)),
            dma((GROUPS, HALVES)),
            dma((2,)),
            dma((n_lm - 1,)),
            dma,
            dma((n_lm - 1,)),
            dma((n_lm - 1,)),
            pltpu.SemaphoreType.REGULAR((3,)),
        ],
        compiler_params=pltpu.CompilerParams(collective_id=0, has_side_effects=True, vmem_limit_bytes=56 * 2**20),
        name="nystrom",
    )(slab, landmarks, codes.T, exponents, eigvec.T, ritz.reshape(1, n_ritz))
    return extended.T


def solution(mesh):
    return jax.shard_map(
        local,
        mesh=mesh,
        in_specs=(
            P("sl", None),
            P(("lm", "sl"), None),
            P(("lm", "sl"), None),
            P(("lm", "sl")),
            P(),
            P(),
        ),
        out_specs=P("sl", None),
        check_vma=False,
    )
```

```python
import functools
import math

import jax
import jax.numpy as jnp
from jax import lax
from jax.experimental import pallas as pl
from jax.experimental.pallas import tpu as pltpu
from jax.sharding import PartitionSpec as P

MESH = pl.DeviceIdType.MESH
HALVES = 2
QUARTERS = 4
GROUPS = 8
NT = (((1,), (1,)), ((), ()))
NN = (((1,), (0,)), ((), ()))


def group_of(col, rel, half):
    if rel == 0:
        return col
    if rel == 2:
        return 6 + col
    early = (rel == -1) == (half == 0)
    return (2 if early else 3) + 2 * col


def kernel(
    slab_hbm, land_hbm, codes_hbm, exponents_hbm, eigvec_hbm, ritz_hbm, out_ref,
    slab, land, vec, acc, swap_out, swap_in, own_sums, rs_out, rs_in, ag_in, codes, exponents, eigvec, ritz,
    load_sem, slab_sem, own_send, fwd_send, vec_send, land_recv, vec_recv, swap_sem, rs_send, rs_recv, ag_send, ag_recv, near,
):
    rows, feat = slab_hbm.shape
    width = land_hbm.shape[0]
    quarter = width // QUARTERS
    n_lm, n_sl = lax.axis_size("lm"), lax.axis_size("sl")
    chunk = rows // n_lm
    scale = math.log2(math.e) / math.sqrt(feat)

    lm = lax.axis_index("lm")
    sl = lax.axis_index("sl")
    z, x_hi = lm // 2, lm % 2
    y, x_lo, core = sl // 4, (sl // 2) % 2, sl % 2
    x = x_hi * 2 + x_lo
    side = 1 - 2 * core

    def place(dx, dy, dz=0, flip=0):
        px = lax.rem(x + dx + 4, 4)
        py = lax.rem(y + dy + 4, 4)
        pz = lax.rem(z + dz + 4, 4)
        pc = lax.rem(core + flip, 2)
        return (pz * 2 + px // 2, py * 4 + lax.rem(px, 2) * 2 + pc)

    def peer(r):
        return (lax.rem(lm + r, n_lm), sl)

    up, down, across, partner = place(0, 1), place(0, -1), place(side, 0), place(0, 0, 0, 1)
    ring = [across, place(-side, 0), place(0, 0, 1), place(0, 0, -1)]

    def greet(semaphore, devices):
        for device in devices:
            pl.semaphore_signal(semaphore, inc=1, device_id=device, device_id_type=MESH)

    barrier = pltpu.get_barrier_semaphore()
    greeted = ring + [up, down, partner]
    greet(barrier, greeted)
    loads = [
        pltpu.make_async_copy(src, dst, load_sem.at[i])
        for i, (src, dst) in enumerate((
            (codes_hbm, codes), (eigvec_hbm, eigvec), (exponents_hbm, exponents), (ritz_hbm, ritz),
            (land_hbm, land.at[0]), (slab_hbm, slab.at[pl.ds(0, rows)]),
        ))
    ]
    for load in loads:
        load.start()
    pl.semaphore_wait(barrier, len(greeted))

    def remote(src, dst, send, recv, device):
        return pltpu.make_async_remote_copy(
            src_ref=src, dst_ref=dst, send_sem=send, recv_sem=recv, device_id=device, device_id_type=MESH
        )

    sent = []

    def start(copy):
        copy.start()
        sent.append(copy)

    def quarter_of(g, q):
        return land.at[g, pl.ds(q * quarter, quarter)]

    def own(i):
        for k, (col, rel, device) in enumerate(((1, 0, across), (0, -1, up), (0, 1, down))):
            q = (i + 2) % QUARTERS if rel == 1 else i
            g = group_of(col, rel, q // 2)
            src = land_hbm.at[pl.ds(q * quarter, quarter)]
            start(remote(src, quarter_of(g, q), own_send.at[3 * i + k], land_recv.at[g, q], device))

    n_vec = [0]

    def send_vec(g, half, to_g, device):
        start(remote(vec.at[g, half], vec.at[to_g, half], vec_send.at[n_vec[0]], vec_recv.at[to_g, half], device))
        n_vec[0] += 1

    def arrive_vec(g, half):
        remote(vec.at[g, half], vec.at[g, half], vec_send.at[0], vec_recv.at[g, half], partner).wait_recv()

    own(0)
    swap_slab = remote(slab_hbm, slab.at[pl.ds(rows, rows)], slab_sem.at[0], slab_sem.at[1], partner)
    swap_slab.start()
    for load in loads[:4]:
        load.wait()
    block = codes.shape[1] // HALVES
    for half in range(HALVES):
        grow = jnp.exp2(jnp.full((codes.shape[0], block), exponents[half], jnp.int32).astype(jnp.float32))
        basis = (codes[:, half * block:(half + 1) * block].astype(jnp.float32) * grow).astype(jnp.bfloat16)
        vec[0, half] = lax.dot_general(eigvec[...], basis, NN, preferred_element_type=jnp.float32).astype(jnp.bfloat16)
    for half in range(HALVES):
        for col, rel, device in ((0, -1, up), (0, 1, down), (1, 0, across)):
            send_vec(0, half, group_of(col, rel, half), device)
    for i in range(1, QUARTERS):
        own(i)
    greet(near.at[0], ring)

    n_fwd = [0]

    def arrive(g, q):
        remote(quarter_of(g, q), quarter_of(g, q), fwd_send.at[0], land_recv.at[g, q], partner).wait_recv()

    def forward(g, q, to_g, device):
        start(remote(quarter_of(g, q), quarter_of(to_g, q), fwd_send.at[n_fwd[0]], land_recv.at[to_g, q], device))
        n_fwd[0] += 1

    def multiply(g, n, lo, hi, first=False):
        part_of = slice(lo * rows, hi * rows)
        left = land[g:g + n].reshape(n * width, feat)
        scores = lax.dot_general(left, slab[part_of], NT, preferred_element_type=jnp.float32)
        affinity = jnp.exp2(scores * scale).astype(jnp.bfloat16)
        coeffs = jnp.concatenate([vec[g + i, half] for i in range(n) for half in range(HALVES)], axis=1)
        part = lax.dot_general(coeffs, affinity, NN, preferred_element_type=jnp.float32)
        acc[:, part_of] = part if first else acc[:, part_of] + part

    for load in loads[4:]:
        load.wait()
    multiply(0, 1, 0, 1, first=True)

    for g in (2, 3):
        for half in range(HALVES):
            arrive_vec(g, half)
            send_vec(g, half, g + 2, across)
            if g == 2:
                send_vec(g, half, 6, (up, down)[half])

    def step2(q0, q1):
        arrive(2, q0)
        forward(2, q0, 4, across)
        forward(2, q0, 6, up)
        arrive(2, q1)
        forward(2, q1, 4, across)
        forward(2, q1, 6, down)

    step2(0, 2)
    pl.semaphore_wait(near.at[0], len(ring))
    greet(near.at[1], ring)
    swap_slab.wait_recv()
    multiply(0, 1, 1, 2, first=True)
    step2(1, 3)
    for half in range(HALVES):
        arrive_vec(1, half)
    for q in range(QUARTERS):
        arrive(1, q)
    multiply(1, 2, 0, 2)

    for q0, q1 in ((0, 2), (1, 3)):
        arrive(3, q1)
        forward(3, q1, 5, across)
        arrive(3, q0)
        forward(3, q0, 5, across)
    pl.semaphore_wait(near.at[1], len(ring))
    greet(near.at[2], ring)
    for q in (0, 2, 1, 3):
        arrive(4, q)
    forward(4, 1, 7, up)
    forward(4, 3, 7, down)
    for half in range(HALVES):
        arrive_vec(6, half)
        send_vec(6, half, 7, across)
        arrive_vec(4, half)
    multiply(3, 2, 0, 2)

    for q in (0, 2):
        arrive(6, q)
        forward(6, q, 7, across)
    for half in range(HALVES):
        arrive_vec(5, half)
    for q in (2, 0, 3, 1):
        arrive(5, q)
    for q in (1, 3):
        arrive(6, q)
    multiply(5, 2, 0, 2)

    factor_row = 1.0 / (ritz[...] * math.sqrt(width * n_lm * n_sl))
    n_ritz = factor_row.shape[1]
    diagonal = lax.broadcasted_iota(jnp.int32, (n_ritz, n_ritz), 0) == lax.broadcasted_iota(jnp.int32, (n_ritz, n_ritz), 1)
    factor = jnp.sum(jnp.where(diagonal, factor_row, 0.0), axis=1, keepdims=True)

    for half in range(HALVES):
        arrive_vec(7, half)
    for q in (0, 2, 1, 3):
        arrive(7, q)
    part = n_lm // 2
    mine = (lm // part) * part
    other = part - mine

    def multiply_last(side_at, first_chunk):
        at = pl.ds(pl.multiple_of(side_at * rows + first_chunk * chunk, part * chunk), part * chunk)
        scores = lax.dot_general(land[7], slab[at], NT, preferred_element_type=jnp.float32)
        affinity = jnp.exp2(scores * scale).astype(jnp.bfloat16)
        coeffs = jnp.concatenate([vec[7, half] for half in range(HALVES)], axis=1)
        return acc[:, at] + lax.dot_general(coeffs, affinity, NN, preferred_element_type=jnp.float32)

    swaps = []
    for k, first_chunk in enumerate((other, mine)):
        swap_out[k] = multiply_last(1, first_chunk).astype(swap_out.dtype)
        swaps.append(remote(swap_out.at[k], swap_in.at[k], swap_sem.at[k], swap_sem.at[2 + k], partner))
        swaps[k].start()
    for k, first_chunk in enumerate((other, mine)):
        sums = multiply_last(0, first_chunk)
        if k == 0:
            pl.semaphore_wait(near.at[2], len(ring))
        swaps[k].wait_recv()
        sums = sums + swap_in[k].astype(jnp.float32)
        if k == 1:
            own_sums[...] = jnp.stack([sums[:, n * chunk:(n + 1) * chunk] for n in range(part)])
        for n in range(part):
            j = first_chunk + n
            rs_out[j] = sums[:, n * chunk:(n + 1) * chunk].astype(rs_out.dtype)
        for n in range(k, part):
            j = first_chunk + lax.rem(lm + (3, 2, 1, 0)[n] if k == 0 else lm + n, part)
            d = lax.rem(j - lm + n_lm, n_lm)
            start(remote(rs_out.at[j], rs_in.at[d - 1], rs_send.at[d - 1], rs_recv, (j, sl)))
    piece = own_sums[lax.rem(lm, part)]
    remote(rs_in, rs_in, fwd_send.at[0], rs_recv, partner).wait_recv()
    for r in range(n_lm - 1):
        piece = piece + rs_in[r].astype(jnp.float32)
    ag_in[lm] = (piece * factor).astype(ag_in.dtype)
    gathered = []
    for r in (5, 3, 4, 2, 6, 1, 7):
        copy = remote(ag_in.at[lm], ag_in.at[lm], ag_send.at[r - 1], ag_recv.at[r - 1], peer(r))
        copy.start()
        gathered.append(copy)
    for copy in gathered:
        copy.wait_recv()
    for j in range(n_lm):
        out_ref[:, j * chunk:(j + 1) * chunk] = ag_in[j].astype(out_ref.dtype)

    for copy in sent + gathered + swaps + [swap_slab]:
        copy.wait_send()


def local(slab, landmarks, codes, exponents, eigvec, ritz):
    n_lm = lax.axis_size("lm")
    rows, feat = slab.shape
    width = landmarks.shape[0]
    n_ritz = eigvec.shape[1]
    block = codes.shape[0] // exponents.shape[0]
    chunk = rows // n_lm
    wire = jnp.bfloat16
    dma = pltpu.SemaphoreType.DMA
    extended = pl.pallas_call(
        kernel,
        out_shape=jax.ShapeDtypeStruct((n_ritz, rows), jnp.float32),
        in_specs=[pl.BlockSpec(memory_space=pl.ANY)] * 6,
        out_specs=pl.BlockSpec(memory_space=pltpu.VMEM),
        scratch_shapes=[
            pltpu.VMEM((2 * rows, feat), slab.dtype),
            pltpu.VMEM((GROUPS, width, feat), landmarks.dtype),
            pltpu.VMEM((GROUPS, HALVES, n_ritz, block), jnp.bfloat16),
            pltpu.VMEM((n_ritz, 2 * rows), jnp.float32),
            pltpu.VMEM((HALVES, n_ritz, rows // 2), wire),
            pltpu.VMEM((HALVES, n_ritz, rows // 2), wire),
            pltpu.VMEM((n_lm // 2, n_ritz, chunk), jnp.float32),
            pltpu.VMEM((n_lm, n_ritz, chunk), wire),
            pltpu.VMEM((n_lm - 1, n_ritz, chunk), wire),
            pltpu.VMEM((n_lm, n_ritz, chunk), wire),
            pltpu.VMEM(codes.shape[::-1], codes.dtype),
            pltpu.SMEM(exponents.shape, exponents.dtype),
            pltpu.VMEM(eigvec.shape[::-1], eigvec.dtype),
            pltpu.VMEM((1, n_ritz), ritz.dtype),
            dma((6,)),
            dma((2,)),
            dma((3 * QUARTERS,)),
            dma((16,)),
            dma((14,)),
            dma((GROUPS, QUARTERS)),
            dma((GROUPS, HALVES)),
            dma((4,)),
            dma((n_lm - 1,)),
            dma,
            dma((n_lm - 1,)),
            dma((n_lm - 1,)),
            pltpu.SemaphoreType.REGULAR((3,)),
        ],
        compiler_params=pltpu.CompilerParams(collective_id=0, has_side_effects=True, vmem_limit_bytes=56 * 2**20),
        name="nystrom",
    )(slab, landmarks, codes.T, exponents, eigvec.T, ritz.reshape(1, n_ritz))
    return extended.T


def solution(mesh):
    return jax.shard_map(
        local,
        mesh=mesh,
        in_specs=(
            P("sl", None),
            P(("lm", "sl"), None),
            P(("lm", "sl"), None),
            P(("lm", "sl")),
            P(),
            P(),
        ),
        out_specs=P("sl", None),
        check_vma=False,
    )
```
